128 devices in a mesh: px: 8 (over x, y_lo), pc: 16 (over z, y_hi, core).
Axes of the slice: x: 4, y: 4 (y_hi: 2, y_lo: 2; y = y_hi * 2 + y_lo), z: 4, core: 2. Of those that a mesh axis runs over, the one named last changes fastest.
Arguments:
- field: bfloat16 [64, 512, 1, 1024], P('pc', None, None, 'px'), may hold values from -6 to 6
- cotangent: bfloat16 [64, 512, 1, 1024], P(None, ('px', 'pc')), may hold values from -6 to 6
- kernel_z: bfloat16 [64, 31], P('pc'), may hold values from -1 to 1
- kernel_x: bfloat16 [64, 31], P('pc'), may hold values from -1 to 1
- weight_in: bfloat16 [64, 128], replicated, may hold values from -0.75 to 0.75
- weight_out: bfloat16 [128, 64], replicated, may hold values from -0.5 to 0.5
Outputs:
- result: bfloat16 [64, 512, 1, 1024], P(None, ('px', 'pc'))
- grad_field: bfloat16 [64, 512, 1, 1024], P('pc', None, None, 'px')
- grad_kernel_z: float32 [64, 31], P('pc')
- grad_kernel_x: float32 [64, 31], P('pc')
- grad_weight_in: float32 [64, 128], replicated
- grad_weight_out: float32 [128, 64], replicated
The draws below stay inside these ranges and needn't reach their ends.
All inputs are finite; a program needn't handle non-finite values.
Results may differ from the reference program's by a relative error of at most 0.0097.
Values may be sent and summed in bfloat16 or wider, within the bound.
A program may use at most 128 MiB of HBM per device.

```python
import math
import jax
import jax.numpy as jnp
from jax import lax

C = 64
H = 128
K = 31
Y = 1
X = 1024
Z = 512


def block_scale(own_key, dims, shards, low, high):
    gain, own = 1.0, jax.random.fold_in(own_key, 6)
    for dim, parts in shards:
        draws = jnp.exp(jax.random.uniform(jax.random.fold_in(own, dim), (parts,), jnp.float32, low / len(shards), high / len(shards)))
        gain = gain * jnp.repeat(draws, dims[dim] // parts).reshape([-1 if axis == dim else 1 for axis in range(len(dims))])
    return gain


def normal_values(rng, shape, spread, limit, pieces=(), held_as=jnp.bfloat16):
    entries = jax.random.normal(rng, shape, jnp.float32) * spread
    if len(pieces) > 0:
        entries = block_scale(rng, shape, pieces, -0.22, 0.18) * entries
    return jnp.clip(entries, min=-limit, max=limit).astype(held_as)


def setup_inputs(seed: int = 0) -> dict:
    arg_keys = jax.random.split(jax.random.key(seed), 7)
    field = normal_values(arg_keys[0], (C, Z, Y, X), 1.0, 6.0, ((0, 16), (3, 8)))
    cotangent = normal_values(arg_keys[1], (C, Z, Y, X), 1.0, 6.0, ((1, 128),))
    kernel_z = normal_values(arg_keys[2], (C, K), K ** -0.5, 1.0, ((0, 16),))
    kernel_x = normal_values(arg_keys[3], (C, K), K ** -0.5, 1.0, ((0, 16),))
    weight_in = normal_values(arg_keys[4], (C, H), C ** -0.5, 0.75)
    weight_out = normal_values(arg_keys[5], (H, C), H ** -0.5, 0.5)
    return {"field": field, "cotangent": cotangent, "kernel_z": kernel_z, "kernel_x": kernel_x, "weight_in": weight_in, "weight_out": weight_out}


def pad_axis(values, axis_pos, rim_width):
    widths = [(0, 0)] * values.ndim
    widths[axis_pos] = (rim_width, rim_width)
    return jnp.pad(values, widths)

def depth_conv(values, kernel, axis_pos):
    channels, depth, rows, width = values.shape
    rim_width = kernel.shape[1] // 2
    if axis_pos == 1:
        flat = values.reshape(channels, depth, rows * width)
        numbers = lax.ConvDimensionNumbers(lhs_spec=(2, 0, 1), rhs_spec=(0, 1, 2), out_spec=(2, 0, 1))
    else:
        flat = values.reshape(channels, depth * rows, width)
        numbers = lax.ConvDimensionNumbers(lhs_spec=(1, 0, 2), rhs_spec=(0, 1, 2), out_spec=(1, 0, 2))
    taps_f = kernel.astype(jnp.float32).reshape(channels, 1, kernel.shape[1])
    output = lax.conv_general_dilated(flat.astype(jnp.float32), taps_f, (1,), [(rim_width, rim_width)], dimension_numbers=numbers, feature_group_count=channels, precision=lax.Precision.HIGHEST, preferred_element_type=jnp.float32)
    return output.reshape(values.shape)

def tap_sums(factor, padded, axis_pos, length):
    taps = padded.shape[axis_pos] - length + 1

    def one_channel(couple):
        grad_c = couple[0].astype(jnp.float32)
        pad_c = couple[1]
        windows = jnp.stack([lax.slice_in_dim(pad_c, tap_idx, tap_idx + length, axis=axis_pos - 1).astype(jnp.float32).reshape(-1) for tap_idx in range(taps)], axis=0)
        return jnp.dot(windows, grad_c.reshape(-1), precision=lax.Precision.HIGHEST, preferred_element_type=jnp.float32)
    return lax.map(one_channel, (factor, padded))

def gelu_tanh(values):
    return jax.nn.gelu(values, approximate=True)

def mlp_pass(mixed, cotangent, weight_in, weight_out):
    as_float = mixed.astype(jnp.float32)
    centre = lax.optimization_barrier(jnp.mean(as_float, axis=0, keepdims=True))
    shifted = as_float - centre
    inv_std = lax.rsqrt(lax.optimization_barrier(jnp.mean(shifted * shifted, axis=0, keepdims=True)) + 1e-06)
    normed = shifted * inv_std
    normed_low = normed.astype(jnp.bfloat16)
    w_in = weight_in.astype(jnp.float32)
    w_out = weight_out.astype(jnp.float32)
    hidden = jnp.einsum('ch,czyx->hzyx', w_in, normed_low.astype(jnp.float32))
    activated, gelu_back = jax.vjp(gelu_tanh, hidden)
    act_low = activated.astype(jnp.bfloat16)
    result = (as_float + jnp.einsum('hc,hzyx->czyx', w_out, act_low.astype(jnp.float32))).astype(jnp.bfloat16)
    cot_f = cotangent.astype(jnp.float32)
    grad_act = jnp.einsum('hc,czyx->hzyx', w_out, cot_f)
    grad_hidden = gelu_back(grad_act)[0].astype(jnp.bfloat16)
    grad_hid_f = grad_hidden.astype(jnp.float32)
    grad_w_out = jnp.einsum('hzyx,czyx->hc', act_low.astype(jnp.float32), cot_f)
    grad_w_in = jnp.einsum('czyx,hzyx->ch', normed_low.astype(jnp.float32), grad_hid_f)
    grad_normed = jnp.einsum('ch,hzyx->czyx', w_in, grad_hid_f)
    average = lax.optimization_barrier(jnp.mean(grad_normed, axis=0, keepdims=True))
    project = lax.optimization_barrier(jnp.mean(grad_normed * normed, axis=0, keepdims=True))
    back_grad = (cot_f + inv_std * (grad_normed - average - normed * project)).astype(jnp.bfloat16)
    return (result, back_grad, grad_w_in, grad_w_out)

def reference(field, cotangent, kernel_z, kernel_x, weight_in, weight_out):
    rim_width = K // 2
    grad_scale = 1.0 / math.sqrt(Y * Z * X)
    along_z = depth_conv(field, kernel_z, 1).astype(jnp.bfloat16)
    padded_a = pad_axis(along_z, 3, rim_width)
    mixed_x = depth_conv(along_z, kernel_x, 3).astype(jnp.bfloat16)
    block_len = math.gcd(Z, 32)
    block_count = Z // block_len

    def to_blocks(values):
        return jnp.moveaxis(values.reshape(C, block_count, block_len, Y, X), 1, 0)

    def from_blocks(values):
        return jnp.moveaxis(values, 0, 1).reshape(C, Z, Y, X)

    def one_block(pair):
        return mlp_pass(pair[0], pair[1], weight_in, weight_out)
    result_b, back_b, grad_in_b, grad_out_b = lax.map(one_block, (to_blocks(mixed_x), to_blocks(cotangent)))
    result = from_blocks(result_b)
    back_grad = from_blocks(back_b)
    grad_a = depth_conv(back_grad, kernel_x[:, ::-1], 3).astype(jnp.bfloat16)
    grad_kernel_x = tap_sums(back_grad, padded_a, 3, X) * grad_scale
    grad_field = depth_conv(grad_a, kernel_z[:, ::-1], 1).astype(jnp.bfloat16)
    grad_kernel_z = tap_sums(grad_a, pad_axis(field, 1, rim_width), 1, Z) * grad_scale
    grad_weight_in = lax.optimization_barrier(jnp.sum(grad_in_b, axis=0)) * grad_scale
    grad_weight_out = lax.optimization_barrier(jnp.sum(grad_out_b, axis=0)) * grad_scale
    return (result, grad_field, grad_kernel_z, grad_kernel_x, grad_weight_in, grad_weight_out)
```

```python
import functools
import math

import jax
import jax.numpy as jnp
from jax import lax
from jax.experimental import pallas as pl
from jax.experimental.pallas import tpu as pltpu
from jax.sharding import PartitionSpec as P

MESH = pl.DeviceIdType.MESH
BF = jnp.bfloat16
F32 = jnp.float32
GELU_A = math.sqrt(2.0 / math.pi)
GELU_B = 0.044715
CHUNKS = 2
SUB = 256


def mm(left, right):
    return lax.dot_general(left, right, (((1,), (0,)), ((), ())), preferred_element_type=F32)


def mm_nt(left, right):
    return lax.dot_general(left, right, (((1,), (1,)), ((), ())), preferred_element_type=F32)


def iota(shape, dim):
    return lax.broadcasted_iota(jnp.int32, shape, dim)


def ones_where(mask):
    return jnp.where(mask, 1.0, 0.0).astype(BF)


def band(row, rows):
    wide = jnp.broadcast_to(row, (rows, 256))
    return pltpu.roll(wide, 241, axis=1, stride=1, stride_axis=0)


def lag_row(product):
    rolled = pltpu.roll(product, 144, axis=1, stride=1, stride_axis=0)
    return jnp.sum(rolled, axis=0, keepdims=True)[:, :128]


def ext_rows(pieces):
    zero = jnp.zeros((64, 128), BF)
    columns = []
    for blk in range(4):
        after = pieces[2 * blk + 2] if blk < 3 else zero
        before = pieces[2 * blk - 1] if blk > 0 else zero
        columns.append(jnp.concatenate([pieces[2 * blk], pieces[2 * blk + 1], after, before], axis=0))
    return jnp.concatenate(columns, axis=1)


def ext_lanes(pieces):
    zero = jnp.zeros((64, 128), BF)
    low = iota((64, 128), 1) < 64
    rows = []
    for blk in range(8):
        after = pieces[blk + 1] if blk < 7 else zero
        before = pieces[blk - 1] if blk > 0 else zero
        edge = jnp.where(low, after, before)
        rows.append(jnp.concatenate([pieces[blk], edge], axis=1))
    return jnp.concatenate(rows, axis=0)


class Exchange:
    def __init__(self, axis, size, me, send, recv, base):
        self.axis, self.size, self.me = axis, size, me
        self.send, self.recv, self.base = send, recv, base
        self.copies = []

    def start(self, src_at, dst_at):
        for k in range(1, self.size):
            peer = lax.rem(self.me + k, self.size)
            copy = pltpu.make_async_remote_copy(
                src_ref=src_at(peer),
                dst_ref=dst_at(self.me),
                send_sem=self.send.at[self.base + k - 1],
                recv_sem=self.recv.at[self.base + k - 1],
                device_id={self.axis: peer},
                device_id_type=MESH,
            )
            copy.start()
            self.copies.append(copy)

    def wait(self):
        for copy in self.copies:
            copy.wait()


def kernel(
    npx, npc, scale,
    field, cot, taps, w_in, w_ot,
    res_out, gf_out, w_out, k_out,
    fe, bands, xs, xr, xe, mx, ss, sr, mixd, cotp, resp, bkp, bs, br, gbx, gs, gr,
    wacc, rs1, rs2, rs2s, wfin, kxp, kxr, kzp, kzr,
    send, recv,
):
    px = lax.axis_index("px")
    pc = lax.axis_index("pc")
    lanes = 1024 // CHUNKS

    barrier = pltpu.get_barrier_semaphore()
    for k in range(1, npx):
        pl.semaphore_signal(barrier, inc=1, device_id={"px": lax.rem(px + k, npx)}, device_id_type=MESH)
    for k in range(1, npc):
        pl.semaphore_signal(barrier, inc=1, device_id={"pc": lax.rem(pc + k, npc)}, device_id_type=MESH)

    base = [0]

    def px_exchange():
        made = Exchange("px", npx, px, send, recv, base[0])
        base[0] += npx - 1
        return made

    def pc_exchange():
        made = Exchange("pc", npc, pc, send, recv, base[0])
        base[0] += npc - 1
        return made

    first = [px_exchange() for _ in range(4)]
    for c in range(4):
        ext = ext_rows([field[c, 64 * q : 64 * q + 64, :] for q in range(8)])
        fe[c] = ext
        made = mm(band(taps[c : c + 1, :], 128).astype(BF), ext).astype(BF)
        for blk in range(4):
            for half in range(2):
                xs[2 * blk + half, c] = made[64 * half : 64 * half + 64, 128 * blk : 128 * blk + 128]
        if c == 0:
            pl.semaphore_wait(barrier, npx + npc - 2)
        first[c].start(lambda peer: xs.at[peer, c], lambda slot: xr.at[slot, c])
    xr[px] = xs[px]

    for c in range(4):
        bands[c] = band(taps[12 + c : 13 + c, :], 256)[:, :128].astype(BF)
        bands[4 + c] = band(taps[8 + c : 9 + c, :], 256)[:, :128].astype(BF)
    shape = (256, 256)
    row, col = iota(shape, 0), iota(shape, 1)
    to_dest = ones_where(col == ((row // 4) % 4) * 64 + (row // 16) * 4 + row % 4)
    from_dest = ones_where(row == ((col // 4) % 4) * 64 + (col // 16) * 4 + col % 4)
    to_cells = ones_where(col == (row % 64) * 4 + row // 64)
    from_cells = ones_where(row == (col % 64) * 4 + col // 64)
    eye = ones_where(iota((128, 128), 0) == iota((128, 128), 1))
    flip = ones_where(iota((128, 128), 0) + iota((128, 128), 1) == 127)
    for part in range(4):
        at = slice(256 * part, 256 * part + 256)
        cotp[:, at] = mm(to_cells, cot[:, at]).astype(BF)
    w_in_v = w_in[...]
    w_ot_v = w_ot[...]
    w_in_t = mm_nt(eye, w_in_v).astype(BF)
    w_o_v = mm_nt(eye, w_ot_v).astype(BF)
    wacc[...] = jnp.zeros_like(wacc)

    for c in range(4):
        first[c].wait()
        ext = ext_lanes([xr[b, c] for b in range(8)])
        xe[c] = ext
        made = mm(ext, bands[c]).astype(BF)
        for b in range(8):
            mx[64 * c : 64 * c + 64, 128 * b : 128 * b + 128] = made[64 * b : 64 * b + 64, :]

    second = [pc_exchange() for _ in range(CHUNKS)]
    for h in range(CHUNKS):
        made = mm(to_dest, mx[:, lanes * h : lanes * h + lanes]).astype(BF)
        ss[h] = made.reshape(npc, 16, lanes)
        second[h].start(lambda peer: ss.at[h, peer], lambda slot: sr.at[h, slot])
        sr[h, pc] = ss[h, pc]

    third = [pc_exchange() for _ in range(CHUNKS)]
    for h in range(CHUNKS):
        second[h].wait()
        mixd[...] = mm(to_cells, sr[h].reshape(256, lanes)).astype(BF)

        def cells(step, carry):
            zz = step // (lanes // SUB)
            part = lax.rem(step, lanes // SUB)
            rows = pl.ds(pl.multiple_of(zz * 64, 64), 64)
            here = pl.ds(pl.multiple_of(part * SUB, SUB), SUB)
            there = pl.ds(pl.multiple_of(lanes * h + part * SUB, SUB), SUB)
            mixed = mixd[rows, here].astype(F32)
            cot_b = cotp[rows, there]
            centre = jnp.mean(mixed, axis=0, keepdims=True)
            shifted = mixed - centre
            inv_std = lax.rsqrt(jnp.mean(shifted * shifted, axis=0, keepdims=True) + 1e-06)
            normed = shifted * inv_std
            low = normed.astype(BF)
            v = mm(w_in_t, low)
            grad_act = mm(w_o_v, cot_b)
            v2 = v * v
            u = v * (GELU_A + (GELU_A * GELU_B) * v2)
            gate = 0.5 + 0.5 * jnp.tanh(u)
            act = v * gate
            slope = 2.0 * GELU_A + (6.0 * GELU_A * GELU_B) * v2
            act_low = act.astype(BF)
            grad_hid = (grad_act * (gate + act * (1.0 - gate) * slope)).astype(BF)
            resp[rows, here] = (mixed + mm(w_ot_v, act_low)).astype(BF)
            grad_n = mm(w_in_v, grad_hid)
            average = jnp.mean(grad_n, axis=0, keepdims=True)
            project = jnp.mean(grad_n * normed, axis=0, keepdims=True)
            bkp[rows, here] = (
                cot_b.astype(F32) + inv_std * (grad_n - average - normed * project)
            ).astype(BF)
            wacc[0:64, :] += mm_nt(cot_b, act_low)
            wacc[64:128, :] += mm_nt(low, grad_hid)
            return carry

        lax.fori_loop(0, 4 * (lanes // SUB), cells, 0)
        bs[h] = mm(from_cells, bkp[...]).astype(BF).reshape(npc, 16, lanes)
        third[h].start(lambda peer: bs.at[h, peer], lambda slot: br.at[h, slot])
        br[h, pc] = bs[h, pc]
        res_out[:, lanes * h : lanes * h + lanes] = mm(from_cells, resp[...]).astype(BF)

    wide1 = pc_exchange()
    wide1.start(lambda peer: wacc.at[pl.ds(pl.multiple_of(peer * 8, 8), 8)], lambda slot: rs1.at[slot])
    rs1[pc] = wacc[pl.ds(pl.multiple_of(pc * 8, 8), 8), :]

    for h in range(CHUNKS):
        third[h].wait()
        gbx[:, lanes * h : lanes * h + lanes] = mm(from_dest, br[h].reshape(256, lanes)).astype(BF)

    wide1.wait()
    rs2s[...] = jnp.sum(rs1[...], axis=0)
    wide2 = px_exchange()
    wide2.start(lambda peer: rs2s, lambda slot: rs2.at[slot])
    rs2[px] = rs2s[...]

    fourth = [px_exchange() for _ in range(4)]
    for c in range(4):
        pieces = [gbx[64 * c : 64 * c + 64, 128 * b : 128 * b + 128] for b in range(8)]
        made = mm(ext_lanes(pieces), bands[4 + c]).astype(BF)
        for b in range(8):
            gs[b, c] = made[64 * b : 64 * b + 64, :]
        fourth[c].start(lambda peer: gs.at[peer, c], lambda slot: gr.at[slot, c])
    gr[px] = gs[px]

    kxp[...] = jnp.zeros_like(kxp)
    for c in range(4):
        stacked = jnp.concatenate(
            [gbx[64 * c : 64 * c + 64, 128 * b : 128 * b + 128] for b in range(8)], axis=0
        )
        turned = mm_nt(flip, stacked).astype(BF)
        kxp[c : c + 1, :] = lag_row(mm(turned, xe[c]))
    kx_ex = px_exchange()
    kx_ex.start(lambda peer: kxp, lambda slot: kxr.at[slot])
    kxr[px] = kxp[...]

    wide2.wait()
    mine = pl.ds(pl.multiple_of(pc * 8, 8), 8)
    wfin[mine, :] = jnp.sum(rs2[...], axis=0) * scale
    wide3 = pc_exchange()
    wide3.start(lambda peer: wfin.at[mine], lambda slot: wfin.at[pl.ds(pl.multiple_of(slot * 8, 8), 8)])

    kzp[...] = jnp.zeros_like(kzp)
    exts = []
    for c in range(4):
        fourth[c].wait()
        ext = ext_rows([gr[q, c] for q in range(8)])
        exts.append(ext)
        turned = mm(flip, ext[:128, :]).astype(BF)
        kzp[c : c + 1, :] = lag_row(mm_nt(turned, fe[c]))
    kz_ex = px_exchange()
    kz_ex.start(lambda peer: kzp, lambda slot: kzr.at[slot])
    kzr[px] = kzp[...]
    for c in range(4):
        made = mm(band(taps[4 + c : 5 + c, :], 128).astype(BF), exts[c]).astype(BF)
        for blk in range(4):
            gf_out[c, 128 * blk : 128 * blk + 128, :] = made[:, 128 * blk : 128 * blk + 128]
    wide3.wait()
    w_out[...] = wfin[...]
    kx_ex.wait()
    k_out[0:8, :] = jnp.sum(kxr[...], axis=0) * scale
    kz_ex.wait()
    k_out[8:16, :] = jnp.sum(kzr[...], axis=0) * scale


def local(npx, npc, field, cotangent, kernel_z, kernel_x, weight_in, weight_out):
    lanes = 1024 // CHUNKS
    pad = [(0, 0), (0, 256 - 31)]
    taps = jnp.concatenate(
        [jnp.pad(k, pad) for k in (kernel_z, kernel_z[:, ::-1], kernel_x, kernel_x[:, ::-1])], axis=0
    ).astype(F32)
    copies = (4 + 4 + 1 + 1 + 1) * (npx - 1) + (2 * CHUNKS + 2) * (npc - 1)
    vmem = pl.BlockSpec(memory_space=pltpu.VMEM)
    scale = 1.0 / math.sqrt(512 * 1024)
    res, gf, w, k = pl.pallas_call(
        functools.partial(kernel, npx, npc, scale),
        out_shape=(
            jax.ShapeDtypeStruct((256, 1024), BF),
            jax.ShapeDtypeStruct((4, 512, 128), BF),
            jax.ShapeDtypeStruct((128, 128), F32),
            jax.ShapeDtypeStruct((16, 128), F32),
        ),
        in_specs=[vmem] * 5,
        out_specs=(vmem,) * 4,
        scratch_shapes=[
            pltpu.VMEM((4, 256, 512), BF),
            pltpu.VMEM((8, 256, 128), BF),
            pltpu.VMEM((8, 4, 64, 128), BF),
            pltpu.VMEM((8, 4, 64, 128), BF),
            pltpu.VMEM((4, 512, 256), BF),
            pltpu.VMEM((256, 1024), BF),
            pltpu.VMEM((CHUNKS, 16, 16, lanes), BF),
            pltpu.VMEM((CHUNKS, 16, 16, lanes), BF),
            pltpu.VMEM((256, lanes), BF),
            pltpu.VMEM((256, 1024), BF),
            pltpu.VMEM((256, lanes), BF),
            pltpu.VMEM((256, lanes), BF),
            pltpu.VMEM((CHUNKS, 16, 16, lanes), BF),
            pltpu.VMEM((CHUNKS, 16, 16, lanes), BF),
            pltpu.VMEM((256, 1024), BF),
            pltpu.VMEM((8, 4, 64, 128), BF),
            pltpu.VMEM((8, 4, 64, 128), BF),
            pltpu.VMEM((128, 128), F32),
            pltpu.VMEM((16, 8, 128), F32),
            pltpu.VMEM((8, 8, 128), F32),
            pltpu.VMEM((8, 128), F32),
            pltpu.VMEM((128, 128), F32),
            pltpu.VMEM((8, 128), F32),
            pltpu.VMEM((8, 8, 128), F32),
            pltpu.VMEM((8, 128), F32),
            pltpu.VMEM((8, 8, 128), F32),
            pltpu.SemaphoreType.DMA((copies,)),
            pltpu.SemaphoreType.DMA((copies,)),
        ],
        compiler_params=pltpu.CompilerParams(
            collective_id=0, has_side_effects=True, vmem_limit_bytes=56 * 1024 * 1024
        ),
    )(
        field.reshape(4, 512, 128),
        cotangent.reshape(256, 1024),
        taps,
        weight_in,
        weight_out.T,
    )
    return (
        res.reshape(64, 4, 1, 1024),
        gf.reshape(4, 512, 1, 128),
        k[8:12, :31],
        k[0:4, :31],
        w[64:128],
        w[0:64].T,
    )


def solution(mesh):
    placed = (
        P("pc", None, None, "px"),
        P(None, ("px", "pc"), None, None),
        P("pc", None),
        P("pc", None),
        P(),
        P(),
    )
    return jax.shard_map(
        functools.partial(local, mesh.shape["px"], mesh.shape["pc"]),
        mesh=mesh,
        in_specs=placed,
        out_specs=(
            P(None, ("px", "pc"), None, None),
            P("pc", None, None, "px"),
            P("pc", None),
            P("pc", None),
            P(),
            P(),
        ),
        check_vma=False,
    )
```

```python
import functools
import math

import jax
import jax.numpy as jnp
from jax import lax
from jax.experimental import pallas as pl
from jax.experimental.pallas import tpu as pltpu
from jax.sharding import PartitionSpec as P

MESH = pl.DeviceIdType.MESH
BF = jnp.bfloat16
F32 = jnp.float32
GELU_A = math.sqrt(2.0 / math.pi)
GELU_B = 0.044715


def mm(left, right):
    return lax.dot_general(left, right, (((1,), (0,)), ((), ())), preferred_element_type=F32)


def mm_nt(left, right):
    return lax.dot_general(left, right, (((1,), (1,)), ((), ())), preferred_element_type=F32)


def iota(shape, dim):
    return lax.broadcasted_iota(jnp.int32, shape, dim)


def ones_where(mask):
    return jnp.where(mask, 1.0, 0.0).astype(BF)


def band(row, rows):
    wide = jnp.broadcast_to(row, (rows, 256))
    return pltpu.roll(wide, 241, axis=1, stride=1, stride_axis=0)


def lag_row(product):
    rolled = pltpu.roll(product, 144, axis=1, stride=1, stride_axis=0)
    return jnp.sum(rolled, axis=0, keepdims=True)[:, :128]


def ext_rows(pieces):
    zero = jnp.zeros((64, 128), BF)
    columns = []
    for blk in range(4):
        after = pieces[2 * blk + 2] if blk < 3 else zero
        before = pieces[2 * blk - 1] if blk > 0 else zero
        columns.append(jnp.concatenate([pieces[2 * blk], pieces[2 * blk + 1], after, before], axis=0))
    return jnp.concatenate(columns, axis=1)


def tile(sheet, c, i):
    return sheet[64 * c : 64 * c + 64, 128 * i : 128 * i + 128]


def stack_lanes(sheet, edges, c):
    return jnp.concatenate(
        [jnp.concatenate([tile(sheet, c, i), tile(edges, c, i)], axis=1) for i in range(8)], axis=0
    )


class Exchange:
    def __init__(self, axis, size, me, send, recv, base):
        self.axis, self.size, self.me = axis, size, me
        self.send, self.recv, self.base = send, recv, base
        self.copies = []

    def start(self, src_at, dst_at):
        for k in range(1, self.size):
            peer = lax.rem(self.me + k, self.size)
            copy = pltpu.make_async_remote_copy(
                src_ref=src_at(peer),
                dst_ref=dst_at(self.me),
                send_sem=self.send.at[self.base + k - 1],
                recv_sem=self.recv.at[self.base + k - 1],
                device_id={self.axis: peer},
                device_id_type=MESH,
            )
            copy.start()
            self.copies.append(copy)

    def wait(self):
        for copy in self.copies:
            copy.wait()


def kernel(
    npx, npc, scale,
    field, cot, taps, w_in, w_ot,
    res_out, gf_out, w_out, k_out,
    fe, bands, az, hs, hr, xe, mx, ss, sr, mixd, cotp, resp, bkp, bs, br, gbx, hs2, hr2,
    wacc, rs1, rs2, rs2s, wfin, kp, kr,
    send, recv, all_send, all_recv, halo_send, halo_recv,
):
    px = lax.axis_index("px")
    pc = lax.axis_index("pc")

    barrier = pltpu.get_barrier_semaphore()

    def greet(k, carry):
        peer = lax.rem(px * npc + pc + k, npx * npc)
        pl.semaphore_signal(
            barrier, inc=1, device_id=(peer // npc, lax.rem(peer, npc)), device_id_type=MESH
        )
        return carry

    lax.fori_loop(1, npx * npc, greet, 0)

    base = [0]

    def px_exchange():
        made = Exchange("px", npx, px, send, recv, base[0])
        base[0] += npx - 1
        return made

    def pc_exchange():
        made = Exchange("pc", npc, pc, send, recv, base[0])
        base[0] += npc - 1
        return made

    def spread(which, step, direction, src, dst):
        peer_px = lax.rem(px + npx + direction * step, npx)
        slot = which * npx + step

        def one(k, carry):
            peer_pc = lax.rem(pc + k, npc)
            pltpu.make_async_remote_copy(
                src_ref=src.at[peer_px, peer_pc],
                dst_ref=dst.at[px, pc],
                send_sem=all_send.at[slot],
                recv_sem=all_recv.at[slot],
                device_id=(peer_px, peer_pc),
                device_id_type=MESH,
            ).start()
            return carry

        if step == 0:
            pltpu.make_async_copy(src.at[px, pc], dst.at[px, pc], all_recv.at[slot]).start()
        lax.fori_loop(1 if step == 0 else 0, npc, one, 0)

    def spread_arrived(which, step, direction, dst):
        from_px = lax.rem(px + npx - direction * step, npx)
        slot = which * npx + step
        whole = dst.at[from_px]
        pltpu.make_async_copy(whole, whole, all_recv.at[slot]).wait()
        return from_px

    def spread_left(which, step, src):
        slot = which * npx + step
        whole = src.at[0] if step else src.at[0, pl.ds(0, npc - 1)]
        pltpu.make_async_copy(whole, whole, all_send.at[slot]).wait()

    def halo_start(which, sheet, pick, out, into):
        packed = mm(sheet[...], pick).astype(BF)
        copies = []
        for side in range(2):
            out[side] = packed[:, 128 * side : 128 * side + 128]
            copy = pltpu.make_async_remote_copy(
                src_ref=out.at[side],
                dst_ref=into.at[side],
                send_sem=halo_send.at[2 * which + side],
                recv_sem=halo_recv.at[2 * which + side],
                device_id={"px": lax.rem(px + (npx - 1 if side == 0 else 1), npx)},
                device_id_type=MESH,
            )
            copy.start()
            copies.append(copy)
        return copies

    def halo_end(copies, pick, into):
        for copy in copies:
            copy.wait()
        keep_after = jnp.where(px < npx - 1, 1.0, 0.0).astype(F32)
        keep_before = jnp.where(px > 0, 1.0, 0.0).astype(F32)
        after = (into[0].astype(F32) * keep_after).astype(BF)
        before = (into[1].astype(F32) * keep_before).astype(BF)
        return mm_nt(jnp.concatenate([after, before], axis=1), pick).astype(BF)

    for c in range(4):
        ext = ext_rows([field[c, 64 * q : 64 * q + 64, :] for q in range(8)])
        fe[c] = ext
        made = mm(band(taps[c : c + 1, :], 128).astype(BF), ext).astype(BF)
        for blk in range(4):
            for half in range(2):
                i = 2 * blk + half
                az[64 * c : 64 * c + 64, 128 * i : 128 * i + 128] = made[
                    64 * half : 64 * half + 64, 128 * blk : 128 * blk + 128
                ]
    row, col = iota((1024, 256), 0), iota((1024, 256), 1)
    pick = ones_where(
        (row // 128 == (col % 128) // 16) & (row % 128 == col % 16 + jnp.where(col < 128, 0, 112))
    )
    pl.semaphore_wait(barrier, npx * npc - 1)
    halo = halo_start(0, az, pick, hs, hr)

    for c in range(4):
        bands[c] = band(taps[12 + c : 13 + c, :], 256)[:, :128].astype(BF)
        bands[4 + c] = band(taps[8 + c : 9 + c, :], 256)[:, :128].astype(BF)
    shape = (256, 256)
    row, col = iota(shape, 0), iota(shape, 1)
    to_dest = ones_where(col == ((row // 4) % 4) * 64 + (row // 16) * 4 + row % 4)
    from_dest = ones_where(row == ((col // 4) % 4) * 64 + (col // 16) * 4 + col % 4)
    to_cells = ones_where(col == (row % 64) * 4 + row // 64)
    from_cells = ones_where(row == (col % 64) * 4 + col // 64)
    eye = ones_where(iota((128, 128), 0) == iota((128, 128), 1))
    flip = ones_where(iota((128, 128), 0) + iota((128, 128), 1) == 127)
    for part in range(4):
        made = mm(to_cells, cot[:, 256 * part : 256 * part + 256]).astype(BF)
        cotp[2 * part] = made[:, :128]
        cotp[2 * part + 1] = made[:, 128:]
    w_in_v = w_in[...]
    w_ot_v = w_ot[...]
    w_in_t = mm_nt(eye, w_in_v).astype(BF)
    w_o_v = mm_nt(eye, w_ot_v).astype(BF)
    wacc[...] = jnp.zeros_like(wacc)

    edges = halo_end(halo, pick, hr)
    for c in range(4):
        ext = stack_lanes(az, edges, c)
        xe[c] = ext
        made = mm(ext, bands[c]).astype(BF)
        for i in range(8):
            mx[64 * c : 64 * c + 64, 128 * i : 128 * i + 128] = made[64 * i : 64 * i + 64, :]

    for part in range(4):
        made = mm(to_dest, mx[:, 256 * part : 256 * part + 256]).astype(BF)
        ss[2 * part] = made[:, :128].reshape(npc, 16, 128)
        ss[2 * part + 1] = made[:, 128:].reshape(npc, 16, 128)
    for step in range(npx):
        spread(0, step, -1, ss, sr)

    for pair in range(4):
        i0 = spread_arrived(0, 2 * pair, -1, sr)
        i1 = spread_arrived(0, 2 * pair + 1, -1, sr)
        both = jnp.concatenate([sr[i0].reshape(256, 128), sr[i1].reshape(256, 128)], axis=1)
        mixd[...] = mm(to_cells, both).astype(BF)

        def cells(zz, carry):
            rows = pl.ds(pl.multiple_of(zz * 64, 64), 64)
            mixed = mixd[rows, :].astype(F32)
            cot_b = jnp.concatenate([cotp[i0, rows, :], cotp[i1, rows, :]], axis=1)
            centre = jnp.mean(mixed, axis=0, keepdims=True)
            shifted = mixed - centre
            inv_std = lax.rsqrt(jnp.mean(shifted * shifted, axis=0, keepdims=True) + 1e-06)
            normed = shifted * inv_std
            low = normed.astype(BF)
            v = mm(w_in_t, low)
            grad_act = mm(w_o_v, cot_b)
            v2 = v * v
            u = v * (GELU_A + (GELU_A * GELU_B) * v2)
            gate = 0.5 + 0.5 * jnp.tanh(u)
            act = v * gate
            slope = 2.0 * GELU_A + (6.0 * GELU_A * GELU_B) * v2
            act_low = act.astype(BF)
            grad_hid = (grad_act * (gate + act * (1.0 - gate) * slope)).astype(BF)
            resp[rows, :] = (mixed + mm(w_ot_v, act_low)).astype(BF)
            grad_n = mm(w_in_v, grad_hid)
            average = jnp.mean(grad_n, axis=0, keepdims=True)
            project = jnp.mean(grad_n * normed, axis=0, keepdims=True)
            bkp[rows, :] = (
                cot_b.astype(F32) + inv_std * (grad_n - average - normed * project)
            ).astype(BF)
            wacc[0:64, :] += mm_nt(cot_b, act_low)
            wacc[64:128, :] += mm_nt(low, grad_hid)
            return carry

        lax.fori_loop(0, 4, cells, 0)
        made = mm(from_cells, bkp[...]).astype(BF)
        bs[i0] = made[:, :128].reshape(npc, 16, 128)
        bs[i1] = made[:, 128:].reshape(npc, 16, 128)
        spread(1, 2 * pair, 1, bs, br)
        spread(1, 2 * pair + 1, 1, bs, br)
        made = mm(from_cells, resp[...]).astype(BF)
        res_out[:, pl.ds(pl.multiple_of(i0 * 128, 128), 128)] = made[:, :128]
        res_out[:, pl.ds(pl.multiple_of(i1 * 128, 128), 128)] = made[:, 128:]

    wide1 = pc_exchange()
    wide1.start(lambda peer: wacc.at[pl.ds(pl.multiple_of(peer * 8, 8), 8)], lambda slot: rs1.at[slot])
    rs1[pc] = wacc[pl.ds(pl.multiple_of(pc * 8, 8), 8), :]

    for pair in range(4):
        i0 = spread_arrived(1, 2 * pair, 1, br)
        i1 = spread_arrived(1, 2 * pair + 1, 1, br)
        both = jnp.concatenate([br[i0].reshape(256, 128), br[i1].reshape(256, 128)], axis=1)
        made = mm(from_dest, both).astype(BF)
        gbx[:, pl.ds(pl.multiple_of(i0 * 128, 128), 128)] = made[:, :128]
        gbx[:, pl.ds(pl.multiple_of(i1 * 128, 128), 128)] = made[:, 128:]
    halo = halo_start(1, gbx, pick, hs2, hr2)

    wide1.wait()
    rs2s[...] = jnp.sum(rs1[...], axis=0)
    wide2 = px_exchange()
    wide2.start(lambda peer: rs2s, lambda slot: rs2.at[slot])
    rs2[px] = rs2s[...]

    kp[...] = jnp.zeros_like(kp)
    for c in range(4):
        stacked = jnp.concatenate([tile(gbx, c, i) for i in range(8)], axis=0)
        turned = mm_nt(flip, stacked).astype(BF)
        kp[c : c + 1, :] = lag_row(mm(turned, xe[c]))

    edges = halo_end(halo, pick, hr2)
    exts = []
    for c in range(4):
        made = mm(stack_lanes(gbx, edges, c), bands[4 + c]).astype(BF)
        ext = ext_rows([made[64 * q : 64 * q + 64, :] for q in range(8)])
        exts.append(ext)
        turned = mm(flip, ext[:128, :]).astype(BF)
        kp[4 + c : 5 + c, :] = lag_row(mm_nt(turned, fe[c]))
    k_ex = px_exchange()
    k_ex.start(lambda peer: kp, lambda slot: kr.at[slot])
    kr[px] = kp[...]

    wide2.wait()
    mine = pl.ds(pl.multiple_of(pc * 8, 8), 8)
    wfin[mine, :] = jnp.sum(rs2[...], axis=0) * scale
    wide3 = pc_exchange()
    wide3.start(lambda peer: wfin.at[mine], lambda slot: wfin.at[pl.ds(pl.multiple_of(slot * 8, 8), 8)])

    for c in range(4):
        made = mm(band(taps[4 + c : 5 + c, :], 128).astype(BF), exts[c]).astype(BF)
        for blk in range(4):
            gf_out[c, 128 * blk : 128 * blk + 128, :] = made[:, 128 * blk : 128 * blk + 128]
    for step in range(npx):
        spread_left(0, step, ss)
        spread_left(1, step, bs)
    k_ex.wait()
    k_out[...] = jnp.sum(kr[...], axis=0) * scale
    wide3.wait()
    w_out[...] = wfin[...]


def local(npx, npc, field, cotangent, kernel_z, kernel_x, weight_in, weight_out):
    pad = [(0, 0), (0, 256 - 31)]
    taps = jnp.concatenate(
        [jnp.pad(k, pad) for k in (kernel_z, kernel_z[:, ::-1], kernel_x, kernel_x[:, ::-1])], axis=0
    ).astype(F32)
    copies = 2 * (npx - 1) + 2 * (npc - 1)
    vmem = pl.BlockSpec(memory_space=pltpu.VMEM)
    scale = 1.0 / math.sqrt(512 * 1024)
    res, gf, w, k = pl.pallas_call(
        functools.partial(kernel, npx, npc, scale),
        out_shape=(
            jax.ShapeDtypeStruct((256, 1024), BF),
            jax.ShapeDtypeStruct((4, 512, 128), BF),
            jax.ShapeDtypeStruct((128, 128), F32),
            jax.ShapeDtypeStruct((8, 128), F32),
        ),
        in_specs=[vmem] * 5,
        out_specs=(vmem,) * 4,
        scratch_shapes=[
            pltpu.VMEM((4, 256, 512), BF),
            pltpu.VMEM((8, 256, 128), BF),
            pltpu.VMEM((256, 1024), BF),
            pltpu.VMEM((2, 256, 128), BF),
            pltpu.VMEM((2, 256, 128), BF),
            pltpu.VMEM((4, 512, 256), BF),
            pltpu.VMEM((256, 1024), BF),
            pltpu.VMEM((8, 16, 16, 128), BF),
            pltpu.VMEM((8, 16, 16, 128), BF),
            pltpu.VMEM((256, 256), BF),
            pltpu.VMEM((8, 256, 128), BF),
            pltpu.VMEM((256, 256), BF),
            pltpu.VMEM((256, 256), BF),
            pltpu.VMEM((8, 16, 16, 128), BF),
            pltpu.VMEM((8, 16, 16, 128), BF),
            pltpu.VMEM((256, 1024), BF),
            pltpu.VMEM((2, 256, 128), BF),
            pltpu.VMEM((2, 256, 128), BF),
            pltpu.VMEM((128, 128), F32),
            pltpu.VMEM((16, 8, 128), F32),
            pltpu.VMEM((8, 8, 128), F32),
            pltpu.VMEM((8, 128), F32),
            pltpu.VMEM((128, 128), F32),
            pltpu.VMEM((8, 128), F32),
            pltpu.VMEM((8, 8, 128), F32),
            pltpu.SemaphoreType.DMA((copies,)),
            pltpu.SemaphoreType.DMA((copies,)),
            pltpu.SemaphoreType.DMA((2 * npx,)),
            pltpu.SemaphoreType.DMA((2 * npx,)),
            pltpu.SemaphoreType.DMA((4,)),
            pltpu.SemaphoreType.DMA((4,)),
        ],
        compiler_params=pltpu.CompilerParams(
            collective_id=0, has_side_effects=True, vmem_limit_bytes=56 * 1024 * 1024
        ),
    )(
        field.reshape(4, 512, 128),
        cotangent.reshape(256, 1024),
        taps,
        weight_in,
        weight_out.T,
    )
    return (
        res.reshape(64, 4, 1, 1024),
        gf.reshape(4, 512, 1, 128),
        k[4:8, :31],
        k[0:4, :31],
        w[64:128],
        w[0:64].T,
    )


def solution(mesh):
    placed = (
        P("pc", None, None, "px"),
        P(None, ("px", "pc"), None, None),
        P("pc", None),
        P("pc", None),
        P(),
        P(),
    )
    return jax.shard_map(
        functools.partial(local, mesh.shape["px"], mesh.shape["pc"]),
        mesh=mesh,
        in_specs=placed,
        out_specs=(
            P(None, ("px", "pc"), None, None),
            P("pc", None, None, "px"),
            P("pc", None),
            P("pc", None),
            P(),
            P(),
        ),
        check_vma=False,
    )
```

```python
import functools
import math

import jax
import jax.numpy as jnp
from jax import lax
from jax.experimental import pallas as pl
from jax.experimental.pallas import tpu as pltpu
from jax.sharding import PartitionSpec as P

MESH = pl.DeviceIdType.MESH
BF = jnp.bfloat16
F32 = jnp.float32
GELU_A = math.sqrt(2.0 / math.pi)
GELU_B = 0.044715


def mm(left, right):
    return lax.dot_general(left, right, (((1,), (0,)), ((), ())), preferred_element_type=F32)


def mm_nt(left, right):
    return lax.dot_general(left, right, (((1,), (1,)), ((), ())), preferred_element_type=F32)


def iota(shape, dim):
    return lax.broadcasted_iota(jnp.int32, shape, dim)


def ones_where(mask):
    return jnp.where(mask, 1.0, 0.0).astype(BF)


def band(row, rows):
    wide = jnp.broadcast_to(row, (rows, 256))
    return pltpu.roll(wide, 241, axis=1, stride=1, stride_axis=0)


def lag_row(product):
    rolled = pltpu.roll(product, 144, axis=1, stride=1, stride_axis=0)
    return jnp.sum(rolled, axis=0, keepdims=True)[:, :128]


def ext_rows(pieces):
    zero = jnp.zeros((64, 128), BF)
    columns = []
    for blk in range(4):
        after = pieces[2 * blk + 2] if blk < 3 else zero
        before = pieces[2 * blk - 1] if blk > 0 else zero
        columns.append(jnp.concatenate([pieces[2 * blk], pieces[2 * blk + 1], after, before], axis=0))
    return jnp.concatenate(columns, axis=1)


def tile(sheet, c, i):
    return sheet[64 * c : 64 * c + 64, 128 * i : 128 * i + 128]


def stack_lanes(sheet, edges, c):
    return jnp.concatenate(
        [jnp.concatenate([tile(sheet, c, i), tile(edges, c, i)], axis=1) for i in range(8)], axis=0
    )


class Exchange:
    def __init__(self, axis, size, me, send, recv, base):
        self.axis, self.size, self.me = axis, size, me
        self.send, self.recv, self.base = send, recv, base
        self.copies = []

    def start(self, src_at, dst_at):
        for k in range(1, self.size):
            peer = lax.rem(self.me + k, self.size)
            copy = pltpu.make_async_remote_copy(
                src_ref=src_at(peer),
                dst_ref=dst_at(self.me),
                send_sem=self.send.at[self.base + k - 1],
                recv_sem=self.recv.at[self.base + k - 1],
                device_id={self.axis: peer},
                device_id_type=MESH,
            )
            copy.start()
            self.copies.append(copy)

    def wait(self):
        for copy in self.copies:
            copy.wait()


def kernel(
    npx, npc, scale,
    field, cot, kz, kx, w_in, w_ot,
    res_out, gf_out, kz_out, kx_out, wi_out, wo_out,
    taps, fs, kfe, bands, az, aze, hs, hr, xe, mx, ss, sr, mixd, cotp, resp, bkp, bs, br, gbx, hs2, hr2,
    wacc, rs1, rs2, rs2s, wfin, kp, kr,
    send, recv, all_send, all_recv, halo_send, halo_recv,
):
    px = lax.axis_index("px")
    pc = lax.axis_index("pc")

    barrier = pltpu.get_barrier_semaphore()

    def greet(k, carry):
        peer = lax.rem(px * npc + pc + k, npx * npc)
        pl.semaphore_signal(
            barrier, inc=1, device_id=(peer // npc, lax.rem(peer, npc)), device_id_type=MESH
        )
        return carry

    lax.fori_loop(1, npx * npc, greet, 0)

    base = [0]

    def px_exchange():
        made = Exchange("px", npx, px, send, recv, base[0])
        base[0] += npx - 1
        return made

    def pc_exchange():
        made = Exchange("pc", npc, pc, send, recv, base[0])
        base[0] += npc - 1
        return made

    def spread(which, step, direction, src, dst):
        peer_px = lax.rem(px + npx + direction * step, npx)
        slot = which * npx + step

        def one(k, carry):
            peer_pc = lax.rem(pc + k, npc)
            pltpu.make_async_remote_copy(
                src_ref=src.at[peer_px, peer_pc],
                dst_ref=dst.at[px, pc],
                send_sem=all_send.at[slot],
                recv_sem=all_recv.at[slot],
                device_id=(peer_px, peer_pc),
                device_id_type=MESH,
            ).start()
            return carry

        if step == 0:
            pltpu.make_async_copy(src.at[px, pc], dst.at[px, pc], all_recv.at[slot]).start()
        lax.fori_loop(1 if step == 0 else 0, npc, one, 0)

    def spread_arrived(which, step, direction, dst):
        from_px = lax.rem(px + npx - direction * step, npx)
        slot = which * npx + step
        whole = dst.at[from_px]
        pltpu.make_async_copy(whole, whole, all_recv.at[slot]).wait()
        return from_px

    def spread_left(which, step, src):
        slot = which * npx + step
        whole = src.at[0] if step else src.at[0, pl.ds(0, npc - 1)]
        pltpu.make_async_copy(whole, whole, all_send.at[slot]).wait()

    def halo_start(which, packed, out, into):
        copies = []
        for side in range(2):
            out[side] = packed[:, 128 * side : 128 * side + 128]
            copy = pltpu.make_async_remote_copy(
                src_ref=out.at[side],
                dst_ref=into.at[side],
                send_sem=halo_send.at[2 * which + side],
                recv_sem=halo_recv.at[2 * which + side],
                device_id={"px": lax.rem(px + (npx - 1 if side == 0 else 1), npx)},
                device_id_type=MESH,
            )
            copy.start()
            copies.append(copy)
        return copies

    def halo_end(copies, pick, into):
        for copy in copies:
            copy.wait()
        keep_after = jnp.where(px < npx - 1, 1.0, 0.0).astype(F32)
        keep_before = jnp.where(px > 0, 1.0, 0.0).astype(F32)
        after = (into[0].astype(F32) * keep_after).astype(BF)
        before = (into[1].astype(F32) * keep_before).astype(BF)
        return mm_nt(jnp.concatenate([after, before], axis=1), pick).astype(BF)

    taps[...] = jnp.zeros_like(taps)
    taps[0:4, 0:31] = kz[...].astype(F32)
    taps[8:12, 0:31] = kx[...].astype(F32)
    back = ones_where(iota((128, 128), 0) + iota((128, 128), 1) == 30)
    turned = mm(taps[:, 0:128].astype(BF), back)
    taps[4:8, 0:128] = turned[0:4]
    taps[12:16, 0:128] = turned[8:12]

    row, col = iota((1024, 256), 0), iota((1024, 256), 1)
    pick = ones_where(
        (row // 128 == (col % 128) // 16) & (row % 128 == col % 16 + jnp.where(col < 128, 0, 112))
    )
    for c in range(4):
        for i in range(8):
            fs[64 * c : 64 * c + 64, 128 * i : 128 * i + 128] = field[c, 64 * i : 64 * i + 64, :]
    packed = mm(fs[...], pick).astype(BF)

    def along_z(sheet, into):
        for c in range(4):
            ext = ext_rows([tile(sheet, c, i) for i in range(8)])
            made = mm(band(taps[c : c + 1, :], 128).astype(BF), ext).astype(BF)
            for i in range(8):
                half = 64 * (i % 2)
                into[64 * c : 64 * c + 64, 128 * i : 128 * i + 128] = made[
                    half : half + 64, 128 * (i // 2) : 128 * (i // 2) + 128
                ]

    for c in range(4):
        bands[c] = band(taps[12 + c : 13 + c, :], 256)[:, :128].astype(BF)
        bands[4 + c] = band(taps[8 + c : 9 + c, :], 256)[:, :128].astype(BF)
    pl.semaphore_wait(barrier, npx * npc - 1)
    halo = halo_start(0, packed, hs, hr)
    along_z(fs, az)

    shape = (256, 256)
    row, col = iota(shape, 0), iota(shape, 1)
    to_dest = ones_where(col == ((row // 4) % 4) * 64 + (row // 16) * 4 + row % 4)
    from_dest = ones_where(row == ((col // 4) % 4) * 64 + (col // 16) * 4 + col % 4)
    to_cells = ones_where(col == (row % 64) * 4 + row // 64)
    from_cells = ones_where(row == (col % 64) * 4 + col // 64)
    eye = ones_where(iota((128, 128), 0) == iota((128, 128), 1))
    flip = ones_where(iota((128, 128), 0) + iota((128, 128), 1) == 127)
    for part in range(4):
        flat = cot[:, :, 256 * part : 256 * part + 256].astype(F32).reshape(256, 256).astype(BF)
        made = mm(to_cells, flat).astype(BF)
        cotp[2 * part] = made[:, :128]
        cotp[2 * part + 1] = made[:, 128:]
    w_in_v = w_in[...]
    w_ot_v = w_ot[...]
    w_in_t = mm_nt(eye, w_in_v).astype(BF)
    w_o_v = mm_nt(eye, w_ot_v).astype(BF)
    wacc[...] = jnp.zeros_like(wacc)

    edges = halo_end(halo, pick, hr)
    along_z(edges, aze)
    for c in range(4):
        ext = stack_lanes(az, aze, c)
        xe[c] = ext
        made = mm(ext, bands[c]).astype(BF)
        for i in range(8):
            mx[64 * c : 64 * c + 64, 128 * i : 128 * i + 128] = made[64 * i : 64 * i + 64, :]

    for part in range(4):
        made = mm(to_dest, mx[:, 256 * part : 256 * part + 256]).astype(BF)
        ss[2 * part] = made[:, :128].reshape(npc, 16, 128)
        ss[2 * part + 1] = made[:, 128:].reshape(npc, 16, 128)
    for step in range(npx):
        spread(0, step, -1, ss, sr)

    for c in range(4):
        made = mm(stack_lanes(fs, edges, c), bands[c]).astype(BF)
        kfe[c] = ext_rows([made[64 * i : 64 * i + 64, :] for i in range(8)])

    for pair in range(4):
        i0 = spread_arrived(0, 2 * pair, -1, sr)
        i1 = spread_arrived(0, 2 * pair + 1, -1, sr)
        both = jnp.concatenate([sr[i0].reshape(256, 128), sr[i1].reshape(256, 128)], axis=1)
        mixd[...] = mm(to_cells, both).astype(BF)

        def cells(zz, carry):
            rows = pl.ds(pl.multiple_of(zz * 64, 64), 64)
            mixed = mixd[rows, :].astype(F32)
            cot_b = jnp.concatenate([cotp[i0, rows, :], cotp[i1, rows, :]], axis=1)
            centre = jnp.mean(mixed, axis=0, keepdims=True)
            shifted = mixed - centre
            inv_std = lax.rsqrt(jnp.mean(shifted * shifted, axis=0, keepdims=True) + 1e-06)
            normed = shifted * inv_std
            low = normed.astype(BF)
            v = mm(w_in_t, low)
            grad_act = mm(w_o_v, cot_b)
            v2 = v * v
            u = v * (GELU_A + (GELU_A * GELU_B) * v2)
            gate = 0.5 + 0.5 * jnp.tanh(u)
            act = v * gate
            slope = 2.0 * GELU_A + (6.0 * GELU_A * GELU_B) * v2
            act_low = act.astype(BF)
            grad_hid = (grad_act * (gate + act * (1.0 - gate) * slope)).astype(BF)
            resp[rows, :] = (mixed + mm(w_ot_v, act_low)).astype(BF)
            grad_n = mm(w_in_v, grad_hid)
            average = jnp.mean(grad_n, axis=0, keepdims=True)
            project = jnp.mean(grad_n * normed, axis=0, keepdims=True)
            bkp[rows, :] = (
                cot_b.astype(F32) + inv_std * (grad_n - average - normed * project)
            ).astype(BF)
            wacc[0:64, :] += mm_nt(cot_b, act_low)
            wacc[64:128, :] += mm_nt(low, grad_hid)
            return carry

        lax.fori_loop(0, 4, cells, 0)
        made = mm(from_cells, bkp[...]).astype(BF)
        bs[i0] = made[:, :128].reshape(npc, 16, 128)
        bs[i1] = made[:, 128:].reshape(npc, 16, 128)
        spread(1, 2 * pair, 1, bs, br)
        spread(1, 2 * pair + 1, 1, bs, br)
        made = mm(from_cells, resp[...]).reshape(64, 4, 256).astype(BF)
        res_out[:, :, pl.ds(pl.multiple_of(i0 * 128, 128), 128)] = made[:, :, :128]
        res_out[:, :, pl.ds(pl.multiple_of(i1 * 128, 128), 128)] = made[:, :, 128:]

    wide1 = pc_exchange()
    wide1.start(lambda peer: wacc.at[pl.ds(pl.multiple_of(peer * 8, 8), 8)], lambda slot: rs1.at[slot])
    rs1[pc] = wacc[pl.ds(pl.multiple_of(pc * 8, 8), 8), :]

    for pair in range(4):
        i0 = spread_arrived(1, 2 * pair, 1, br)
        i1 = spread_arrived(1, 2 * pair + 1, 1, br)
        both = jnp.concatenate([br[i0].reshape(256, 128), br[i1].reshape(256, 128)], axis=1)
        made = mm(from_dest, both).astype(BF)
        gbx[:, pl.ds(pl.multiple_of(i0 * 128, 128), 128)] = made[:, :128]
        gbx[:, pl.ds(pl.multiple_of(i1 * 128, 128), 128)] = made[:, 128:]
    halo = halo_start(1, mm(gbx[...], pick).astype(BF), hs2, hr2)

    wide1.wait()
    rs2s[...] = jnp.sum(rs1[...], axis=0)
    wide2 = px_exchange()
    wide2.start(lambda peer: rs2s, lambda slot: rs2.at[slot])
    rs2[px] = rs2s[...]

    for c in range(4):
        pieces = [tile(gbx, c, i) for i in range(8)]
        turned = mm_nt(flip, jnp.concatenate(pieces, axis=0)).astype(BF)
        kp[c : c + 1, :] = lag_row(mm(turned, xe[c]))
        blocks = [jnp.concatenate(pieces[2 * b : 2 * b + 2], axis=0) for b in range(4)]
        turned = mm(flip, jnp.concatenate(blocks, axis=1)).astype(BF)
        kp[4 + c : 5 + c, :] = lag_row(mm_nt(turned, kfe[c]))
    k_ex = px_exchange()
    k_ex.start(lambda peer: kp, lambda slot: kr.at[slot])
    kr[px] = kp[...]

    wide2.wait()
    mine = pl.ds(pl.multiple_of(pc * 8, 8), 8)
    wfin[mine, :] = jnp.sum(rs2[...], axis=0) * scale
    wide3 = pc_exchange()
    wide3.start(lambda peer: wfin.at[mine], lambda slot: wfin.at[pl.ds(pl.multiple_of(slot * 8, 8), 8)])

    edges = halo_end(halo, pick, hr2)
    exts = []
    for c in range(4):
        made = mm(stack_lanes(gbx, edges, c), bands[4 + c]).astype(BF)
        exts.append(ext_rows([made[64 * q : 64 * q + 64, :] for q in range(8)]))
    for c in range(4):
        made = mm(band(taps[4 + c : 5 + c, :], 128).astype(BF), exts[c]).astype(BF)
        for blk in range(4):
            gf_out[c, 128 * blk : 128 * blk + 128, :] = made[:, 128 * blk : 128 * blk + 128]
    for step in range(npx):
        spread_left(0, step, ss)
        spread_left(1, step, bs)
    k_ex.wait()
    total = jnp.sum(kr[...], axis=0) * scale
    kx_out[...] = total[0:4, :31]
    kz_out[...] = total[4:8, :31]
    wide3.wait()
    wo_out[...] = wfin[0:64, :]
    wi_out[...] = wfin[64:128, :]


def write_kernel(*refs):
    half = len(refs) // 2
    for source, target in zip(refs[:half], refs[half:]):
        target[...] = source[...]


def local(npx, npc, field, cotangent, kernel_z, kernel_x, weight_in, weight_out):
    copies = 2 * (npx - 1) + 2 * (npc - 1)
    vmem = pl.BlockSpec(memory_space=pltpu.VMEM)
    scale = 1.0 / math.sqrt(512 * 1024)
    made = pl.pallas_call(
        functools.partial(kernel, npx, npc, scale),
        out_shape=(
            jax.ShapeDtypeStruct((64, 4, 1024), BF),
            jax.ShapeDtypeStruct((4, 512, 128), BF),
            jax.ShapeDtypeStruct((4, 31), F32),
            jax.ShapeDtypeStruct((4, 31), F32),
            jax.ShapeDtypeStruct((64, 128), F32),
            jax.ShapeDtypeStruct((64, 128), F32),
        ),
        in_specs=[vmem] * 6,
        out_specs=(vmem,) * 6,
        scratch_shapes=[
            pltpu.VMEM((16, 256), F32),
            pltpu.VMEM((256, 1024), BF),
            pltpu.VMEM((4, 256, 512), BF),
            pltpu.VMEM((8, 256, 128), BF),
            pltpu.VMEM((256, 1024), BF),
            pltpu.VMEM((256, 1024), BF),
            pltpu.VMEM((2, 256, 128), BF),
            pltpu.VMEM((2, 256, 128), BF),
            pltpu.VMEM((4, 512, 256), BF),
            pltpu.VMEM((256, 1024), BF),
            pltpu.VMEM((8, 16, 16, 128), BF),
            pltpu.VMEM((8, 16, 16, 128), BF),
            pltpu.VMEM((256, 256), BF),
            pltpu.VMEM((8, 256, 128), BF),
            pltpu.VMEM((256, 256), BF),
            pltpu.VMEM((256, 256), BF),
            pltpu.VMEM((8, 16, 16, 128), BF),
            pltpu.VMEM((8, 16, 16, 128), BF),
            pltpu.VMEM((256, 1024), BF),
            pltpu.VMEM((2, 256, 128), BF),
            pltpu.VMEM((2, 256, 128), BF),
            pltpu.VMEM((128, 128), F32),
            pltpu.VMEM((16, 8, 128), F32),
            pltpu.VMEM((8, 8, 128), F32),
            pltpu.VMEM((8, 128), F32),
            pltpu.VMEM((128, 128), F32),
            pltpu.VMEM((8, 128), F32),
            pltpu.VMEM((8, 8, 128), F32),
            pltpu.SemaphoreType.DMA((copies,)),
            pltpu.SemaphoreType.DMA((copies,)),
            pltpu.SemaphoreType.DMA((2 * npx,)),
            pltpu.SemaphoreType.DMA((2 * npx,)),
            pltpu.SemaphoreType.DMA((4,)),
            pltpu.SemaphoreType.DMA((4,)),
        ],
        compiler_params=pltpu.CompilerParams(
            collective_id=0, has_side_effects=True, vmem_limit_bytes=56 * 1024 * 1024
        ),
    )(
        field.reshape(4, 512, 128),
        cotangent.reshape(64, 4, 1024),
        kernel_z,
        kernel_x,
        weight_in,
        weight_out.T,
    )
    res, gf, grad_kz, grad_kx, grad_in, grad_out = pl.pallas_call(
        write_kernel,
        out_shape=tuple(jax.ShapeDtypeStruct(m.shape, m.dtype) for m in made),
        in_specs=[vmem] * 6,
        out_specs=(vmem,) * 6,
    )(*made)
    return (
        res.reshape(64, 4, 1, 1024),
        gf.reshape(4, 512, 1, 128),
        grad_kz,
        grad_kx,
        grad_in,
        grad_out.T,
    )


def solution(mesh):
    placed = (
        P("pc", None, None, "px"),
        P(None, ("px", "pc"), None, None),
        P("pc", None),
        P("pc", None),
        P(),
        P(),
    )
    return jax.shard_map(
        functools.partial(local, mesh.shape["px"], mesh.shape["pc"]),
        mesh=mesh,
        in_specs=placed,
        out_specs=(
            P(None, ("px", "pc"), None, None),
            P("pc", None, None, "px"),
            P("pc", None),
            P("pc", None),
            P(),
            P(),
        ),
        check_vma=False,
    )
```

```python
import functools
import math

import jax
import jax.numpy as jnp
from jax import lax
from jax.experimental import pallas as pl
from jax.experimental.pallas import tpu as pltpu
from jax.sharding import PartitionSpec as P

MESH = pl.DeviceIdType.MESH
BF = jnp.bfloat16
F32 = jnp.float32
GELU_A = math.sqrt(2.0 / math.pi)
GELU_B = 0.044715


def mm(left, right):
    return lax.dot_general(left, right, (((1,), (0,)), ((), ())), preferred_element_type=F32)


def mm_nt(left, right):
    return lax.dot_general(left, right, (((1,), (1,)), ((), ())), preferred_element_type=F32)


def iota(shape, dim):
    return lax.broadcasted_iota(jnp.int32, shape, dim)


def ones_where(mask):
    return jnp.where(mask, 1.0, 0.0).astype(BF)


def band(row, rows):
    wide = jnp.broadcast_to(row, (rows, 256))
    return pltpu.roll(wide, 241, axis=1, stride=1, stride_axis=0)


def lag_row(product):
    rolled = pltpu.roll(product, 144, axis=1, stride=1, stride_axis=0)
    return jnp.sum(rolled, axis=0, keepdims=True)[:, :128]


def ext_rows(pieces):
    zero = jnp.zeros((64, 128), BF)
    columns = []
    for blk in range(4):
        after = pieces[2 * blk + 2] if blk < 3 else zero
        before = pieces[2 * blk - 1] if blk > 0 else zero
        columns.append(jnp.concatenate([pieces[2 * blk], pieces[2 * blk + 1], after, before], axis=0))
    return jnp.concatenate(columns, axis=1)


def tile(sheet, c, i):
    return sheet[64 * c : 64 * c + 64, 128 * i : 128 * i + 128]


def stack_lanes(sheet, edges, c):
    return jnp.concatenate(
        [jnp.concatenate([tile(sheet, c, i), tile(edges, c, i)], axis=1) for i in range(8)], axis=0
    )


class Exchange:
    def __init__(self, axis, size, me, send, recv, base):
        self.axis, self.size, self.me = axis, size, me
        self.send, self.recv, self.base = send, recv, base
        self.copies = []

    def start(self, src_at, dst_at):
        for k in range(1, self.size):
            peer = lax.rem(self.me + k, self.size)
            copy = pltpu.make_async_remote_copy(
                src_ref=src_at(peer),
                dst_ref=dst_at(self.me),
                send_sem=self.send.at[self.base + k - 1],
                recv_sem=self.recv.at[self.base + k - 1],
                device_id={self.axis: peer},
                device_id_type=MESH,
            )
            copy.start()
            self.copies.append(copy)

    def wait(self):
        for copy in self.copies:
            copy.wait()


def kernel(
    npx, npc, scale,
    field_h, cot_h, kz_h, kx_h, w_in_h, w_ot_h,
    res_out, gf_out, kz_out, kx_out, wi_out, wo_out,
    field, cot, kz, kx, w_in, w_ot, in_sem,
    taps, fs, kfe, bands, az, aze, hs, hr, xe, mx, ss, sr, mixd, cotp, resp, bkp, bs, br, gbx, hs2, hr2,
    wacc, rs1, rs2, rs2s, wfin, kp, kr,
    send, recv, all_send, all_recv, halo_send, halo_recv,
):
    px = lax.axis_index("px")
    pc = lax.axis_index("pc")

    loads = [
        pltpu.make_async_copy(source, target, in_sem.at[k])
        for k, (source, target) in enumerate(
            ((kz_h, kz), (kx_h, kx), (field_h, field), (w_in_h, w_in), (w_ot_h, w_ot), (cot_h, cot))
        )
    ]
    for load in loads:
        load.start()

    barrier = pltpu.get_barrier_semaphore()

    def greet(k, carry):
        peer = lax.rem(px * npc + pc + k, npx * npc)
        pl.semaphore_signal(
            barrier, inc=1, device_id=(peer // npc, lax.rem(peer, npc)), device_id_type=MESH
        )
        return carry

    lax.fori_loop(1, npx * npc, greet, 0)

    base = [0]

    def px_exchange():
        made = Exchange("px", npx, px, send, recv, base[0])
        base[0] += npx - 1
        return made

    def pc_exchange():
        made = Exchange("pc", npc, pc, send, recv, base[0])
        base[0] += npc - 1
        return made

    def spread(which, step, direction, src, dst):
        peer_px = lax.rem(px + npx + direction * step, npx)
        slot = which * npx + step

        def one(k, carry):
            peer_pc = lax.rem(pc + k, npc)
            pltpu.make_async_remote_copy(
                src_ref=src.at[peer_px, peer_pc],
                dst_ref=dst.at[px, pc],
                send_sem=all_send.at[slot],
                recv_sem=all_recv.at[slot],
                device_id=(peer_px, peer_pc),
                device_id_type=MESH,
            ).start()
            return carry

        if step == 0:
            pltpu.make_async_copy(src.at[px, pc], dst.at[px, pc], all_recv.at[slot]).start()
        lax.fori_loop(1 if step == 0 else 0, npc, one, 0)

    def spread_arrived(which, step, direction, dst):
        from_px = lax.rem(px + npx - direction * step, npx)
        slot = which * npx + step
        whole = dst.at[from_px]
        pltpu.make_async_copy(whole, whole, all_recv.at[slot]).wait()
        return from_px

    def spread_left(which, step, src):
        slot = which * npx + step
        whole = src.at[0] if step else src.at[0, pl.ds(0, npc - 1)]
        pltpu.make_async_copy(whole, whole, all_send.at[slot]).wait()

    def halo_start(which, packed, out, into):
        copies = []
        for side in range(2):
            out[side] = packed[:, 128 * side : 128 * side + 128]
            copy = pltpu.make_async_remote_copy(
                src_ref=out.at[side],
                dst_ref=into.at[side],
                send_sem=halo_send.at[2 * which + side],
                recv_sem=halo_recv.at[2 * which + side],
                device_id={"px": lax.rem(px + (npx - 1 if side == 0 else 1), npx)},
                device_id_type=MESH,
            )
            copy.start()
            copies.append(copy)
        return copies

    def halo_end(copies, pick, into):
        for copy in copies:
            copy.wait()
        keep_after = jnp.where(px < npx - 1, 1.0, 0.0).astype(F32)
        keep_before = jnp.where(px > 0, 1.0, 0.0).astype(F32)
        after = (into[0].astype(F32) * keep_after).astype(BF)
        before = (into[1].astype(F32) * keep_before).astype(BF)
        return mm_nt(jnp.concatenate([after, before], axis=1), pick).astype(BF)

    loads[0].wait()
    loads[1].wait()
    taps[...] = jnp.zeros_like(taps)
    taps[0:4, 0:31] = kz[...].astype(F32)
    taps[8:12, 0:31] = kx[...].astype(F32)
    back = ones_where(iota((128, 128), 0) + iota((128, 128), 1) == 30)
    turned = mm(taps[:, 0:128].astype(BF), back)
    taps[4:8, 0:128] = turned[0:4]
    taps[12:16, 0:128] = turned[8:12]

    row, col = iota((1024, 256), 0), iota((1024, 256), 1)
    pick = ones_where(
        (row // 128 == (col % 128) // 16) & (row % 128 == col % 16 + jnp.where(col < 128, 0, 112))
    )
    loads[2].wait()
    for c in range(4):
        for i in range(8):
            fs[64 * c : 64 * c + 64, 128 * i : 128 * i + 128] = field[c, 64 * i : 64 * i + 64, :]
    packed = mm(fs[...], pick).astype(BF)

    def along_z(sheet, into):
        for c in range(4):
            ext = ext_rows([tile(sheet, c, i) for i in range(8)])
            made = mm(band(taps[c : c + 1, :], 128).astype(BF), ext).astype(BF)
            for i in range(8):
                half = 64 * (i % 2)
                into[64 * c : 64 * c + 64, 128 * i : 128 * i + 128] = made[
                    half : half + 64, 128 * (i // 2) : 128 * (i // 2) + 128
                ]

    for c in range(4):
        bands[c] = band(taps[12 + c : 13 + c, :], 256)[:, :128].astype(BF)
        bands[4 + c] = band(taps[8 + c : 9 + c, :], 256)[:, :128].astype(BF)
    pl.semaphore_wait(barrier, npx * npc - 1)
    halo = halo_start(0, packed, hs, hr)
    along_z(fs, az)

    for load in loads[3:]:
        load.wait()
    shape = (256, 256)
    row, col = iota(shape, 0), iota(shape, 1)
    to_dest = ones_where(col == ((row // 4) % 4) * 64 + (row // 16) * 4 + row % 4)
    from_dest = ones_where(row == ((col // 4) % 4) * 64 + (col // 16) * 4 + col % 4)
    to_cells = ones_where(col == (row % 64) * 4 + row // 64)
    from_cells = ones_where(row == (col % 64) * 4 + col // 64)
    eye = ones_where(iota((128, 128), 0) == iota((128, 128), 1))
    flip = ones_where(iota((128, 128), 0) + iota((128, 128), 1) == 127)
    for part in range(4):
        flat = cot[:, :, 256 * part : 256 * part + 256].astype(F32).reshape(256, 256).astype(BF)
        made = mm(to_cells, flat).astype(BF)
        cotp[2 * part] = made[:, :128]
        cotp[2 * part + 1] = made[:, 128:]
    w_in_v = w_in[...]
    w_ot_v = w_ot[...]
    w_in_t = mm_nt(eye, w_in_v).astype(BF)
    w_o_v = mm_nt(eye, w_ot_v).astype(BF)
    wacc[...] = jnp.zeros_like(wacc)

    edges = halo_end(halo, pick, hr)
    along_z(edges, aze)
    for c in range(4):
        ext = stack_lanes(az, aze, c)
        xe[c] = ext
        made = mm(ext, bands[c]).astype(BF)
        for i in range(8):
            mx[64 * c : 64 * c + 64, 128 * i : 128 * i + 128] = made[64 * i : 64 * i + 64, :]

    for part in range(4):
        made = mm(to_dest, mx[:, 256 * part : 256 * part + 256]).astype(BF)
        ss[2 * part] = made[:, :128].reshape(npc, 16, 128)
        ss[2 * part + 1] = made[:, 128:].reshape(npc, 16, 128)
    for step in range(npx):
        spread(0, step, -1, ss, sr)

    for c in range(4):
        made = mm(stack_lanes(fs, edges, c), bands[c]).astype(BF)
        kfe[c] = ext_rows([made[64 * i : 64 * i + 64, :] for i in range(8)])

    for pair in range(4):
        i0 = spread_arrived(0, 2 * pair, -1, sr)
        i1 = spread_arrived(0, 2 * pair + 1, -1, sr)
        both = jnp.concatenate([sr[i0].reshape(256, 128), sr[i1].reshape(256, 128)], axis=1)
        mixd[...] = mm(to_cells, both).astype(BF)

        def cells(zz, carry):
            rows = pl.ds(pl.multiple_of(zz * 64, 64), 64)
            mixed = mixd[rows, :].astype(F32)
            cot_b = jnp.concatenate([cotp[i0, rows, :], cotp[i1, rows, :]], axis=1)
            centre = jnp.mean(mixed, axis=0, keepdims=True)
            shifted = mixed - centre
            inv_std = lax.rsqrt(jnp.mean(shifted * shifted, axis=0, keepdims=True) + 1e-06)
            normed = shifted * inv_std
            low = normed.astype(BF)
            v = mm(w_in_t, low)
            grad_act = mm(w_o_v, cot_b)
            v2 = v * v
            u = v * (GELU_A + (GELU_A * GELU_B) * v2)
            gate = 0.5 + 0.5 * jnp.tanh(u)
            act = v * gate
            slope = 2.0 * GELU_A + (6.0 * GELU_A * GELU_B) * v2
            act_low = act.astype(BF)
            grad_hid = (grad_act * (gate + act * (1.0 - gate) * slope)).astype(BF)
            resp[rows, :] = (mixed + mm(w_ot_v, act_low)).astype(BF)
            grad_n = mm(w_in_v, grad_hid)
            average = jnp.mean(grad_n, axis=0, keepdims=True)
            project = jnp.mean(grad_n * normed, axis=0, keepdims=True)
            bkp[rows, :] = (
                cot_b.astype(F32) + inv_std * (grad_n - average - normed * project)
            ).astype(BF)
            wacc[0:64, :] += mm_nt(cot_b, act_low)
            wacc[64:128, :] += mm_nt(low, grad_hid)
            return carry

        lax.fori_loop(0, 4, cells, 0, unroll=4)
        made = mm(from_cells, bkp[...]).astype(BF)
        bs[i0] = made[:, :128].reshape(npc, 16, 128)
        bs[i1] = made[:, 128:].reshape(npc, 16, 128)
        spread(1, 2 * pair, 1, bs, br)
        spread(1, 2 * pair + 1, 1, bs, br)
        made = mm(from_cells, resp[...]).reshape(64, 4, 256).astype(BF)
        res_out[:, :, pl.ds(pl.multiple_of(i0 * 128, 128), 128)] = made[:, :, :128]
        res_out[:, :, pl.ds(pl.multiple_of(i1 * 128, 128), 128)] = made[:, :, 128:]

    wide1 = pc_exchange()
    wide1.start(lambda peer: wacc.at[pl.ds(pl.multiple_of(peer * 8, 8), 8)], lambda slot: rs1.at[slot])
    rs1[pc] = wacc[pl.ds(pl.multiple_of(pc * 8, 8), 8), :]

    for pair in range(4):
        i0 = spread_arrived(1, 2 * pair, 1, br)
        i1 = spread_arrived(1, 2 * pair + 1, 1, br)
        both = jnp.concatenate([br[i0].reshape(256, 128), br[i1].reshape(256, 128)], axis=1)
        made = mm(from_dest, both).astype(BF)
        gbx[:, pl.ds(pl.multiple_of(i0 * 128, 128), 128)] = made[:, :128]
        gbx[:, pl.ds(pl.multiple_of(i1 * 128, 128), 128)] = made[:, 128:]
    halo = halo_start(1, mm(gbx[...], pick).astype(BF), hs2, hr2)

    wide1.wait()
    rs2s[...] = jnp.sum(rs1[...], axis=0)
    wide2 = px_exchange()
    wide2.start(lambda peer: rs2s, lambda slot: rs2.at[slot])
    rs2[px] = rs2s[...]

    for c in range(4):
        pieces = [tile(gbx, c, i) for i in range(8)]
        turned = mm_nt(flip, jnp.concatenate(pieces, axis=0)).astype(BF)
        kp[c : c + 1, :] = lag_row(mm(turned, xe[c]))
        blocks = [jnp.concatenate(pieces[2 * b : 2 * b + 2], axis=0) for b in range(4)]
        turned = mm(flip, jnp.concatenate(blocks, axis=1)).astype(BF)
        kp[4 + c : 5 + c, :] = lag_row(mm_nt(turned, kfe[c]))
    k_ex = px_exchange()
    k_ex.start(lambda peer: kp, lambda slot: kr.at[slot])
    kr[px] = kp[...]

    wide2.wait()
    mine = pl.ds(pl.multiple_of(pc * 8, 8), 8)
    wfin[mine, :] = jnp.sum(rs2[...], axis=0) * scale
    wide3 = pc_exchange()
    wide3.start(lambda peer: wfin.at[mine], lambda slot: wfin.at[pl.ds(pl.multiple_of(slot * 8, 8), 8)])

    edges = halo_end(halo, pick, hr2)
    exts = []
    for c in range(4):
        made = mm(stack_lanes(gbx, edges, c), bands[4 + c]).astype(BF)
        exts.append(ext_rows([made[64 * q : 64 * q + 64, :] for q in range(8)]))
    for c in range(4):
        made = mm(band(taps[4 + c : 5 + c, :], 128).astype(BF), exts[c]).astype(BF)
        for blk in range(4):
            gf_out[c, 128 * blk : 128 * blk + 128, :] = made[:, 128 * blk : 128 * blk + 128]
    for step in range(npx):
        spread_left(0, step, ss)
        spread_left(1, step, bs)
    k_ex.wait()
    total = jnp.sum(kr[...], axis=0) * scale
    kx_out[...] = total[0:4, :31]
    kz_out[...] = total[4:8, :31]
    wide3.wait()
    wo_out[...] = wfin[0:64, :]
    wi_out[...] = wfin[64:128, :]


def write_kernel(*refs):
    half = len(refs) // 2
    for source, target in zip(refs[:half], refs[half:]):
        target[...] = source[...]


def local(npx, npc, field, cotangent, kernel_z, kernel_x, weight_in, weight_out):
    copies = 2 * (npx - 1) + 2 * (npc - 1)
    vmem = pl.BlockSpec(memory_space=pltpu.VMEM)
    scale = 1.0 / math.sqrt(512 * 1024)
    made = pl.pallas_call(
        functools.partial(kernel, npx, npc, scale),
        out_shape=(
            jax.ShapeDtypeStruct((64, 4, 1024), BF),
            jax.ShapeDtypeStruct((4, 512, 128), BF),
            jax.ShapeDtypeStruct((4, 31), F32),
            jax.ShapeDtypeStruct((4, 31), F32),
            jax.ShapeDtypeStruct((64, 128), F32),
            jax.ShapeDtypeStruct((64, 128), F32),
        ),
        in_specs=[pl.BlockSpec(memory_space=pltpu.HBM)] * 6,
        out_specs=(vmem,) * 6,
        scratch_shapes=[
            pltpu.VMEM((4, 512, 128), BF),
            pltpu.VMEM((64, 4, 1024), BF),
            pltpu.VMEM((4, 31), BF),
            pltpu.VMEM((4, 31), BF),
            pltpu.VMEM((64, 128), BF),
            pltpu.VMEM((64, 128), BF),
            pltpu.SemaphoreType.DMA((6,)),
            pltpu.VMEM((16, 256), F32),
            pltpu.VMEM((256, 1024), BF),
            pltpu.VMEM((4, 256, 512), BF),
            pltpu.VMEM((8, 256, 128), BF),
            pltpu.VMEM((256, 1024), BF),
            pltpu.VMEM((256, 1024), BF),
            pltpu.VMEM((2, 256, 128), BF),
            pltpu.VMEM((2, 256, 128), BF),
            pltpu.VMEM((4, 512, 256), BF),
            pltpu.VMEM((256, 1024), BF),
            pltpu.VMEM((8, 16, 16, 128), BF),
            pltpu.VMEM((8, 16, 16, 128), BF),
            pltpu.VMEM((256, 256), BF),
            pltpu.VMEM((8, 256, 128), BF),
            pltpu.VMEM((256, 256), BF),
            pltpu.VMEM((256, 256), BF),
            pltpu.VMEM((8, 16, 16, 128), BF),
            pltpu.VMEM((8, 16, 16, 128), BF),
            pltpu.VMEM((256, 1024), BF),
            pltpu.VMEM((2, 256, 128), BF),
            pltpu.VMEM((2, 256, 128), BF),
            pltpu.VMEM((128, 128), F32),
            pltpu.VMEM((16, 8, 128), F32),
            pltpu.VMEM((8, 8, 128), F32),
            pltpu.VMEM((8, 128), F32),
            pltpu.VMEM((128, 128), F32),
            pltpu.VMEM((8, 128), F32),
            pltpu.VMEM((8, 8, 128), F32),
            pltpu.SemaphoreType.DMA((copies,)),
            pltpu.SemaphoreType.DMA((copies,)),
            pltpu.SemaphoreType.DMA((2 * npx,)),
            pltpu.SemaphoreType.DMA((2 * npx,)),
            pltpu.SemaphoreType.DMA((4,)),
            pltpu.SemaphoreType.DMA((4,)),
        ],
        compiler_params=pltpu.CompilerParams(
            collective_id=0, has_side_effects=True, vmem_limit_bytes=56 * 1024 * 1024
        ),
    )(
        field.reshape(4, 512, 128),
        cotangent.reshape(64, 4, 1024),
        kernel_z,
        kernel_x,
        weight_in,
        weight_out.T,
    )
    res, gf, grad_kz, grad_kx, grad_in, grad_out = pl.pallas_call(
        write_kernel,
        out_shape=tuple(jax.ShapeDtypeStruct(m.shape, m.dtype) for m in made),
        in_specs=[vmem] * 6,
        out_specs=(vmem,) * 6,
    )(*made)
    return (
        res.reshape(64, 4, 1, 1024),
        gf.reshape(4, 512, 1, 128),
        grad_kz,
        grad_kx,
        grad_in,
        grad_out.T,
    )


def solution(mesh):
    placed = (
        P("pc", None, None, "px"),
        P(None, ("px", "pc"), None, None),
        P("pc", None),
        P("pc", None),
        P(),
        P(),
    )
    return jax.shard_map(
        functools.partial(local, mesh.shape["px"], mesh.shape["pc"]),
        mesh=mesh,
        in_specs=placed,
        out_specs=(
            P(None, ("px", "pc"), None, None),
            P("pc", None, None, "px"),
            P("pc", None),
            P("pc", None),
            P(),
            P(),
        ),
        check_vma=False,
    )
```
